32 devices in a mesh: dp: 8 (over y, x, core), group: 4 (over z).
Axes of the slice: x: 2, y: 2, z: 4, core: 2. Of those that a mesh axis runs over, the one named last changes fastest.
Arguments:
- frames: bfloat16 [4, 192, 3840], P('group', 'dp'), may hold values from -6 to 6
- lengths: int32 [4, 64], P('group', 'dp'), may hold values from 0 to 144, as said below
- targets: int32 [4, 64], P('group', 'dp'), may hold values from 0 to 7, as said below
- offsets: int32 [4, 64], P('group', 'dp'), may hold values from 0 to 15, as said below
- first_filter: bfloat16 [3, 3, 512], replicated, may hold values from -2 to 2
- second_filter: bfloat16 [3, 3, 512, 512], replicated, may hold values from -0.09375 to 0.09375
- projection: bfloat16 [10240, 1024], P(('dp', 'group')), may hold values from -0.0625 to 0.0625
- pre_gain: float32 [1024], replicated, may hold values from 0.5 to 1.5
- expand_weight: bfloat16 [1024, 2048], replicated, may hold values from -0.1875 to 0.1875
- depth_kernel: float32 [31, 1024], replicated, may hold values from -1 to 1
- mid_gain: float32 [1024], replicated, may hold values from 0.5 to 1.5
- output_weight: bfloat16 [1024, 1024], replicated, may hold values from -0.1875 to 0.1875
- cotangent: bfloat16 [4, 1536, 1024], P('group', 'dp'), may hold values from -0.08984375 to 0.08984375
Outputs:
- encoded: bfloat16 [4, 1536, 1024], P('group', 'dp')
- expand_grad: float32 [1024, 2048], P(('dp', 'group'))
- output_grad: float32 [1024, 1024], P(('dp', 'group'))
- kernel_grad: float32 [31, 1024], P(None, ('dp', 'group'))
- prenorm_grad: float32 [1024], P(('dp', 'group'))
- midnorm_grad: float32 [1024], P(('dp', 'group'))
The draws below stay inside these ranges and needn't reach their ends.
Inputs may be any that keep to these rules, and one draw needn't show every extreme that they name: `lengths`: 0 marks an empty entry. An utterance has n = ceil(length / 48) blocks, at most 3, taking the next n rows of its device's frames in entry order from row 0. `targets`: the 8 entries of one device name every device of its group once. `offsets`: 0 for empty entries. The utterances sent to one device fill its 16 slots exactly, in disjoint runs of consecutive slots; each device receives 8 utterances, each of 1 to 3 blocks.
All inputs are finite; a program needn't handle non-finite values.
Results may differ from the reference program's by a relative error of at most 0.014.
Values may be sent and summed in bfloat16 or wider, within the bound.
A program may use at most 256 MiB of HBM per device.

```python
from functools import partial
import jax
import jax.numpy as jnp
from jax import lax

D = 1024
C = 512
MEL = 80
KW = 31
FB = 48
CAP = 3
R_DEV = 16
PEERS = 8
GROUPS = 4
FS = 12
FQ = 20
ROWS = 192
SLOTS = 24


def plan_group(key):
    pieces = R_DEV // 2
    key_order, key_swing, key_star, key_tail, key_source, key_entry = jax.random.split(key, 6)
    order = jax.vmap(partial(jax.random.permutation, x=pieces))(jax.random.split(key_order, PEERS))
    swing = jax.random.randint(key_swing, (PEERS, pieces), -1, 2)
    star = jax.random.randint(key_star, (), 0, PEERS)
    places = jnp.arange(pieces)
    devices = jnp.arange(PEERS)
    last = pieces - 1
    star_row = jnp.sum(jnp.where(devices[:, None] == star, order, 0), axis=0)
    last_value = jnp.sum(jnp.where(places == last, star_row, 0))
    swapped = jnp.where(star_row == 1, last_value, jnp.where(places == last, 1, star_row))
    order = jnp.where(devices[:, None] == star, swapped[None, :], order)
    pair_value = swing[:, places // 2]
    pair_value = jnp.where((devices[:, None] == star) & (places[None, :] // 2 == 0), 1, pair_value)
    signs = jnp.where(places % 2 == 0, 1, -1)
    paired = places < 2 * (pieces // 2)
    moves = jnp.where(paired[None, :], pair_value * signs[None, :], 0)
    hits = (order[:, :, None] == places[None, None, :]).astype(jnp.int32)
    sizes = 2 + jnp.sum(moves[:, :, None] * hits, axis=1)
    starts = jnp.cumsum(sizes, axis=1) - sizes
    tail = jax.random.randint(key_tail, (PEERS, pieces), 1, FB + 1)
    forced = jnp.sum(jnp.where(places == 0, swapped, 0))
    tail = jnp.where((devices[:, None] == star) & (places[None, :] == forced), FB, tail)
    lengths = (sizes - 1) * FB + tail
    sources = jax.vmap(partial(jax.random.permutation, x=PEERS))(jax.random.split(key_source, PEERS))[:, :pieces]
    entry = jax.vmap(partial(jax.random.permutation, x=PEERS))(jax.random.split(key_entry, PEERS))
    owned = (sources[None, :, :] == devices[:, None, None]).astype(jnp.int32)
    length_pair = jnp.sum(owned * lengths[None, :, :], axis=2)
    start_pair = jnp.sum(owned * starts[None, :, :], axis=2)
    placed = (entry[:, :, None] == devices[None, None, :]).astype(jnp.int32)
    entry_length = jnp.sum(placed * length_pair[:, :, None], axis=1)
    entry_start = jnp.sum(placed * start_pair[:, :, None], axis=1)
    entry_target = jnp.sum(placed * devices[None, :, None], axis=1)
    return (entry_length.reshape(-1).astype(jnp.int32), entry_target.reshape(-1).astype(jnp.int32), entry_start.reshape(-1).astype(jnp.int32))


def plan_tables(key):
    keys = jax.random.split(jax.random.fold_in(key, 7), GROUPS)
    return jax.vmap(plan_group)(keys)


def draw_lengths(key, part):
    return plan_tables(key)[0]


def draw_targets(key, part):
    return plan_tables(key)[1]


def draw_offsets(key, part):
    return plan_tables(key)[2]


def block_levels(key, extent, shards, least, largest):
    level = 1.0
    for axis_at, parts in shards:
        heights = jax.random.uniform(jax.random.fold_in(jax.random.fold_in(key, 6), axis_at), (parts,), jnp.float32, least / len(shards), largest / len(shards))
        level = level * jnp.repeat(jnp.exp(heights), extent[axis_at] // parts).reshape((-1,) + (1,) * (len(extent) - 1 - axis_at))
    return level


def gaussian(rng, dims, scale, reach, cuts=(), held_as=jnp.bfloat16):
    factor_of = block_levels(rng, dims, cuts, -0.22, 0.18) if cuts else 1.0
    result = jax.random.normal(rng, dims, jnp.float32) * scale * factor_of
    return jnp.minimum(jnp.maximum(result, -reach), reach).astype(held_as)


def setup_inputs(seed: int = 0) -> dict:
    streams_of = jax.random.split(jax.random.key(seed), 14)
    return {
        "frames": gaussian(streams_of[0], (GROUPS, PEERS * SLOTS, FB * MEL), 1.0, 6.0, ((0, 4), (1, 8))),
        "lengths": draw_lengths(jax.random.fold_in(streams_of[13], 71), 0),
        "targets": draw_targets(jax.random.fold_in(streams_of[13], 71), 0),
        "offsets": draw_offsets(jax.random.fold_in(streams_of[13], 71), 0),
        "first_filter": gaussian(streams_of[4], (3, 3, C), 9 ** -0.5, 2.0),
        "second_filter": gaussian(streams_of[5], (3, 3, C, C), (9 * C) ** -0.5, 0.09375),
        "projection": gaussian(streams_of[6], (FQ * C, D), (FQ * C) ** -0.5, 0.0625, ((0, 32),)),
        "pre_gain": jnp.clip(1.0 + 0.1 * jax.random.normal(streams_of[7], (D,), jnp.float32), 0.5, 1.5),
        "expand_weight": gaussian(streams_of[8], (D, 2 * D), D ** -0.5, 0.1875),
        "depth_kernel": gaussian(streams_of[9], (KW, D), KW ** -0.5, 1.0, (), jnp.float32),
        "mid_gain": jnp.clip(1.0 + 0.1 * jax.random.normal(streams_of[10], (D,), jnp.float32), 0.5, 1.5),
        "output_weight": gaussian(streams_of[11], (D, D), D ** -0.5, 0.1875),
        "cotangent": gaussian(streams_of[12], (GROUPS, PEERS * ROWS, D), 0.015625, 0.08984375, ((0, 4), (1, 8))),
    }


EPS = 1e-05

def product(left, right):
    return jnp.dot(left.astype(jnp.float32), right.astype(jnp.float32), preferred_element_type=jnp.float32)

def over_rows(left, right):
    return lax.dot_general(left.astype(jnp.float32), right.astype(jnp.float32), (((0,), (0,)), ((), ())), preferred_element_type=jnp.float32)

def against(left, right):
    return lax.dot_general(left.astype(jnp.float32), right.astype(jnp.float32), (((1,), (1,)), ((), ())), preferred_element_type=jnp.float32)

def tap_planes(values, starts):
    half_rows = values.shape[0] // 2
    half_cols = values.shape[1] // 2
    paired = values.reshape((half_rows, 2, half_cols, 2) + values.shape[2:])
    even_rows = paired[:, 0]
    odd_rows = paired[:, 1]
    before = jnp.concatenate([jnp.zeros_like(odd_rows[:1]), odd_rows[:-1]], axis=0)
    shape = (half_rows,) + (1,) * (before.ndim - 1)
    before = jnp.where(starts.reshape(shape), jnp.zeros_like(before), before)
    planes = []
    for source in (before, even_rows, odd_rows):
        even_cols = source[:, :, 0]
        odd_cols = source[:, :, 1]
        left_cols = jnp.concatenate([jnp.zeros_like(odd_cols[:, :1]), odd_cols[:, :-1]], axis=1)
        planes.extend([left_cols, even_cols, odd_cols])
    return planes

def subsample(blocks, valid_frames, is_first, first_filter, second_filter):
    count = blocks.shape[0]
    channels = first_filter.shape[2]
    frame_index = jnp.arange(FB)
    keep_raw = frame_index[None, :] < valid_frames[:, None]
    raw = jnp.where(keep_raw[:, :, None], blocks.reshape(count, FB, MEL), jnp.zeros((), blocks.dtype))
    raw = raw.reshape(count * FB, MEL)
    first_rows = ((frame_index[None, :FB // 2] == 0) & is_first[:, None]).reshape(-1)
    planes = tap_planes(raw, first_rows)
    stacked = jnp.stack(planes, axis=2).reshape(-1, 9)
    level = product(stacked, first_filter.reshape(9, channels))
    level = level.reshape(count * FB // 2, MEL // 2, channels)
    keep_one = (2 * frame_index[None, :FB // 2] < valid_frames[:, None]).reshape(-1)
    level_one = jnp.where(keep_one[:, None, None], jax.nn.relu(level), 0.0).astype(jnp.bfloat16)
    second_rows = ((frame_index[None, :FB // 4] == 0) & is_first[:, None]).reshape(-1)
    planes = tap_planes(level_one, second_rows)
    total = jnp.zeros((count * FB // 4 * (MEL // 4), channels), jnp.float32)
    for number, plane in enumerate(planes):
        total = total + product(plane.reshape(-1, channels), second_filter[number // 3, number % 3])
    keep_two = (4 * frame_index[None, :FB // 4] < valid_frames[:, None]).reshape(-1)
    level_two = jnp.where(keep_two[:, None], jax.nn.relu(total).reshape(count * FB // 4, -1), 0.0).astype(jnp.bfloat16)
    return (level_two, keep_two.astype(jnp.float32))

def standardise(values):
    centered = values - lax.optimization_barrier(jnp.mean(values, axis=1, keepdims=True))
    scale = lax.rsqrt(lax.optimization_barrier(jnp.mean(centered * centered, axis=1, keepdims=True)) + EPS)
    return (centered * scale, scale)

def depth_forward(values, segment, kernel):
    width = kernel.shape[0]
    half = width // 2
    rows = values.shape[0]
    padded = jnp.pad(values, ((half, half), (0, 0)))
    labels = jnp.pad(segment, (half, half), constant_values=-1)
    total = jnp.zeros(values.shape, jnp.float32)
    for offset in range(width):
        same = labels[offset:offset + rows] == segment
        total = total + jnp.where(same[:, None], padded[offset:offset + rows], 0.0) * kernel[offset]
    return total

def depth_backward(values, grad_depth, segment, kernel):
    width = kernel.shape[0]
    half = width // 2
    rows = values.shape[0]
    padded = jnp.pad(values, ((half, half), (0, 0)))
    padded_grad = jnp.pad(grad_depth, ((half, half), (0, 0)))
    labels = jnp.pad(segment, (half, half), constant_values=-1)
    grad_in = jnp.zeros(values.shape, jnp.float32)
    kernel_rows = []
    for offset in range(width):
        same = labels[offset:offset + rows] == segment
        shifted = jnp.where(same[:, None], padded[offset:offset + rows], 0.0)
        kernel_rows.append(lax.optimization_barrier(jnp.sum(shifted * grad_depth, axis=0)))
        back = 2 * half - offset
        same_back = labels[back:back + rows] == segment
        grad_in = grad_in + jnp.where(same_back[:, None], padded_grad[back:back + rows], 0.0) * kernel[offset]
    return (grad_in, jnp.stack(kernel_rows, axis=0))

def module(hidden_in, row_mask, segment, cotangent, pre_gain, expand_weight, depth_kernel, mid_gain, output_weight):
    width = hidden_in.shape[1]
    hidden = hidden_in.astype(jnp.float32)
    normed_in = standardise(hidden)[0]
    norm_in = (normed_in * pre_gain).astype(jnp.bfloat16)
    expanded = product(norm_in, expand_weight)
    value = expanded[:, :width]
    gate = jax.nn.sigmoid(expanded[:, width:])
    gated = value * gate * row_mask[:, None]
    depth_out = depth_forward(gated, segment, depth_kernel)
    normed_mid, scale_mid = standardise(depth_out)
    scaled_mid = normed_mid * mid_gain
    sigma = jax.nn.sigmoid(scaled_mid)
    swish = (scaled_mid * sigma).astype(jnp.bfloat16)
    encoded = ((hidden + product(swish, output_weight)) * row_mask[:, None]).astype(jnp.bfloat16)
    grad_out = jnp.where(row_mask[:, None] > 0, cotangent, jnp.zeros((), cotangent.dtype))
    output_grad = over_rows(swish, grad_out)
    grad_swish = against(grad_out, output_weight)
    grad_scaled = grad_swish * (sigma + scaled_mid * sigma * (1.0 - sigma))
    midnorm_grad = lax.optimization_barrier(jnp.sum(grad_scaled * normed_mid, axis=0))
    excess = grad_scaled * mid_gain
    grad_depth = scale_mid * (excess - lax.optimization_barrier(jnp.mean(excess, axis=1, keepdims=True)) - normed_mid * lax.optimization_barrier(jnp.mean(excess * normed_mid, axis=1, keepdims=True)))
    grad_gated, kernel_grad = depth_backward(gated, grad_depth, segment, depth_kernel)
    grad_gated = grad_gated * row_mask[:, None]
    grad_expanded = jnp.concatenate([grad_gated * gate, grad_gated * value * gate * (1.0 - gate)], axis=1).astype(jnp.bfloat16)
    expand_grad = over_rows(norm_in, grad_expanded)
    grad_norm = against(grad_expanded, expand_weight)
    prenorm_grad = lax.optimization_barrier(jnp.sum(grad_norm * normed_in, axis=0))
    return (encoded, (expand_grad, output_grad, kernel_grad, prenorm_grad, midnorm_grad))

def layout(sizes, routes, starts_at):
    sizes = sizes.reshape(PEERS, PEERS)
    routes = routes.reshape(PEERS, PEERS)
    starts_at = starts_at.reshape(PEERS, PEERS)
    blocks_used = (sizes + FB - 1) // FB
    first_stored = jnp.cumsum(blocks_used, axis=1) - blocks_used
    device = jnp.arange(PEERS, dtype=jnp.int32)[:, None]
    total = PEERS * R_DEV
    source_index = jnp.zeros((total,), jnp.int32)
    valid_frames = jnp.zeros((total,), jnp.int32)
    first_slot = jnp.zeros((total,), jnp.int32)
    for within in range(CAP):
        live = (within < blocks_used) & (sizes > 0)
        place = jnp.where(live, routes * R_DEV + starts_at + within, total).reshape(-1).astype(jnp.int32)
        source_index = source_index.at[place].set((device * SLOTS + first_stored + within).reshape(-1).astype(jnp.int32), mode='drop')
        valid_frames = valid_frames.at[place].set(jnp.clip(sizes - within * FB, 0, FB).reshape(-1).astype(jnp.int32), mode='drop')
        first_slot = first_slot.at[place].set(starts_at.reshape(-1).astype(jnp.int32), mode='drop')
    return (source_index, valid_frames, first_slot)

def take_rows(whole, index):
    return jnp.take(whole, index, axis=0)

def reference(frames, lengths, targets, offsets, first_filter, second_filter, projection, pre_gain, expand_weight, depth_kernel, mid_gain, output_weight, cotangent):
    source_index, valid_frames, first_slot = jax.vmap(layout)(lengths, targets, offsets)
    packed = jax.vmap(take_rows)(frames, source_index)
    blocks = packed.reshape(GROUPS * PEERS, R_DEV, FB * MEL)

    def device_step(carry, item):
        block_rows, valid_row, first_row, cotangent_rows = item
        is_first = first_row == jnp.arange(R_DEV)
        features, row_mask = subsample(block_rows, valid_row, is_first, first_filter, second_filter)
        hidden_in = product(features, projection).astype(jnp.bfloat16)
        segment = jnp.repeat(first_row, FS)
        encoded, grads = module(hidden_in, row_mask, segment, cotangent_rows, pre_gain, expand_weight, depth_kernel, mid_gain, output_weight)
        return (tuple((held + term for held, term in zip(carry, grads))), encoded)
    zeros = (jnp.zeros((D, 2 * D), jnp.float32), jnp.zeros((D, D), jnp.float32), jnp.zeros((KW, D), jnp.float32), jnp.zeros((D,), jnp.float32), jnp.zeros((D,), jnp.float32))
    totals, encoded = lax.scan(device_step, zeros, (blocks, valid_frames.reshape(GROUPS * PEERS, R_DEV), first_slot.reshape(GROUPS * PEERS, R_DEV), cotangent.reshape(GROUPS * PEERS, ROWS, D)))
    return (encoded.reshape(GROUPS, PEERS * ROWS, D), totals[0], totals[1], totals[2], totals[3], totals[4])
```

```python
import functools

import jax
import jax.numpy as jnp
from jax import lax
from jax.experimental import pallas as pl
from jax.experimental.pallas import tpu as pltpu
from jax.sharding import PartitionSpec as P

MEL = 80
FB = 48
CAP = 3
R_DEV = 16
FS = 12


EPS = 1e-05


def product(left, right):
    return jnp.dot(left, right, preferred_element_type=jnp.float32)


def over_rows(left, right):
    return lax.dot_general(
        left, right, (((0,), (0,)), ((), ())), preferred_element_type=jnp.float32
    )


def against(left, right):
    return lax.dot_general(
        left, right, (((1,), (1,)), ((), ())), preferred_element_type=jnp.float32
    )


FC = 4
LANES = 128


def conv_kernel(blocks_ref, valid_ref, first_ref, one_ref, two_ref, out_ref, taps, keep, even, odd):
    step = pl.program_id(0)
    slots = blocks_ref.shape[0]
    rows = slots * FS
    channels = two_ref.shape[2]

    @pl.when(step == 0)
    def _():
        valid = valid_ref[...]
        later = first_ref[...] == 0
        lane = lax.broadcasted_iota(jnp.int32, (slots, 2 * LANES), 1)
        inside = (lane >= 1) & (lane <= MEL)
        pieces = []
        for k in range(FB):
            start = MEL * k
            base = start // LANES * LANES
            if base + 2 * LANES <= FB * MEL:
                window = blocks_ref[:, base : base + 2 * LANES].astype(jnp.float32)
            else:
                tail = blocks_ref[:, base : base + LANES].astype(jnp.float32)
                window = jnp.concatenate([tail, jnp.zeros_like(tail)], axis=1)
            moved = pltpu.roll(window, (1 - (start - base)) % (2 * LANES), 1)
            moved = jnp.where(inside, moved, 0.0)[:, :LANES]
            pieces.append(jnp.where(k < valid, moved, 0.0))
        before = {}
        for back in (1, 2, 3):
            before[-back] = jnp.where(later, pltpu.roll(pieces[FB - back], 1, 0), 0.0)

        def frame(k):
            return before[k] if k < 0 else pieces[k]

        last_valid = pltpu.roll(valid.astype(jnp.float32), 1, 0)
        for kk in range(FS):
            for part, offset in ((0, -3), (1, -1), (2, 1)):
                at = part * rows + kk * slots
                for i in range(3):
                    taps[at : at + slots, i * LANES : (i + 1) * LANES] = frame(
                        4 * kk + offset + i
                    ).astype(jnp.bfloat16)
                if part == 0 and kk == 0:
                    kept = (last_valid > FB - 2.0) & later
                else:
                    kept = 4 * kk + 2 * (part - 1) < valid
                keep[at : at + slots, :] = kept.astype(jnp.float32)
        odd[:, 0] = jnp.zeros(odd.shape[:1] + odd.shape[2:], odd.dtype)

    @pl.when(step > 0)
    def _():
        odd[:, 0] = odd[:, FC]

    picked = lax.broadcasted_iota(jnp.int32, (3 * LANES, LANES), 0)
    column = lax.broadcasted_iota(jnp.int32, (3 * LANES, LANES), 1)
    wanted = jnp.full((3 * LANES, LANES), -4 * MEL, jnp.int32)
    for i in range(3):
        wanted = jnp.where(
            (column >= 5 * i) & (column < 5 * i + 5), i * LANES + column - 5 * i, wanted
        )
    for local in range(FC):
        shift = 4 * (step * FC + local)
        chosen = jnp.where(picked == wanted + shift, 1.0, 0.0).astype(jnp.bfloat16)
        for part in range(3):
            span = slice(part * rows, (part + 1) * rows)
            window = product(taps[span, :], chosen).astype(jnp.bfloat16)
            mask = keep[span, 0:1] > 0
            level = jnp.where(mask, jnp.maximum(product(window, one_ref[...]), 0.0), 0.0).astype(
                jnp.bfloat16
            )
            even[part, local] = level[:, :channels]
            odd[part, local + 1] = level[:, channels:]
    total = jnp.zeros((FC * rows, channels), jnp.float32)
    for i in range(3):
        for j, source in ((0, odd[i, 0:FC]), (1, even[i]), (2, odd[i, 1 : FC + 1])):
            total = total + product(source.reshape(FC * rows, channels), two_ref[3 * i + j])
    mask = keep[rows : 2 * rows, 0:1] > 0
    for local in range(FC):
        part = total[local * rows : (local + 1) * rows]
        out_ref[:, local * channels : (local + 1) * channels] = jnp.where(
            mask, jnp.maximum(part, 0.0), 0.0
        ).astype(jnp.bfloat16)


def subsample(blocks, valid_frames, is_first, first_filter, second_filter):
    slots = blocks.shape[0]
    channels = first_filter.shape[2]
    rows = slots * FS
    bins = MEL // 4
    low = jnp.pad(first_filter, ((0, 0), (0, 2), (0, 0)))
    high = jnp.pad(first_filter, ((0, 0), (2, 0), (0, 0)))
    one = jnp.concatenate([low, high], axis=2).reshape(15, 2 * channels)
    one = jnp.pad(one, ((0, LANES - 15), (0, 0)))
    two = second_filter.reshape(9, channels, channels)
    valid = jnp.broadcast_to(valid_frames[:, None], (slots, LANES))
    first = jnp.broadcast_to(is_first[:, None], (slots, LANES)).astype(jnp.int32)
    whole = lambda shape: pl.BlockSpec(shape, lambda s: (0,) * len(shape))
    features = pl.pallas_call(
        conv_kernel,
        grid=(bins // FC,),
        in_specs=[
            whole(blocks.shape),
            whole(valid.shape),
            whole(first.shape),
            whole(one.shape),
            whole(two.shape),
        ],
        out_specs=pl.BlockSpec((rows, FC * channels), lambda s: (0, s)),
        out_shape=jax.ShapeDtypeStruct((rows, bins * channels), jnp.bfloat16),
        scratch_shapes=[
            pltpu.VMEM((3 * rows, 3 * LANES), jnp.bfloat16),
            pltpu.VMEM((3 * rows, LANES), jnp.float32),
            pltpu.VMEM((3, FC, rows, channels), jnp.bfloat16),
            pltpu.VMEM((3, FC + 1, rows, channels), jnp.bfloat16),
        ],
        compiler_params=pltpu.CompilerParams(vmem_limit_bytes=44 * 2**20),
        cost_estimate=pl.CostEstimate(
            flops=30 * 10**9, bytes_accessed=10 * 2**20, transcendentals=0
        ),
        name="subsample",
    )(blocks, valid, first, one, two)
    keep_two = 4 * jnp.arange(FS)[None, :] < valid_frames[:, None]
    return (features, keep_two.reshape(-1).astype(jnp.float32))


PIECE = 512


def sum_kernel(peers, groups, wide_ref, mid_ref, thin_ref, wide_out, mid_out, thin_out, *rest):
    stages = peers.bit_length() - 1
    got_big = rest[:stages]
    sum_big = rest[stages : 2 * stages]
    got_thin = rest[2 * stages : 3 * stages]
    sum_thin = rest[3 * stages : 4 * stages]
    last_big, last_thin, send_sem, recv_sem = rest[4 * stages : 4 * stages + 4]
    me = lax.axis_index("dp")
    group = lax.axis_index("group")
    bits = [(me // 2**b) % 2 for b in range(stages)]
    partners = [(me + (1 - 2 * bits[b]) * 2**b, group) for b in range(stages)]
    others = [lax.rem(group + s, groups) for s in range(1, groups)]
    barrier = pltpu.get_barrier_semaphore()
    for device in partners + [(me, other) for other in others]:
        pl.semaphore_signal(
            barrier, inc=1, device_id=device, device_id_type=pl.DeviceIdType.MESH
        )
    pl.semaphore_wait(barrier, stages + groups - 1)

    pieces = []
    order = [0] + list(range(1, stages))
    swapped = [0] + list(range(stages - 1, 0, -1))
    at = 0
    for source, out in ((wide_ref, wide_out), (mid_ref, mid_out)):
        for begin in range(0, source.shape[-1], PIECE):
            path = order if len(pieces) % 2 == 0 else swapped
            pieces.append((source, begin, out, begin, got_big, sum_big, last_big, at, PIECE, path))
            at += PIECE
    pieces.append(
        (thin_ref, 0, thin_out, 0, got_thin, sum_thin, last_thin, 0, thin_ref.shape[-1], order)
    )
    pieces = pieces[-1:] + pieces[:-1]
    started = []

    def begin_stage(number, stage):
        source, begin, _, _, got, total, _, at, width, path = pieces[number]
        left = [b for b in range(stages - 1, -1, -1) if b not in path[:stage]]
        place = left.index(path[stage])
        bit = bits[path[stage]]
        ref, column = (source, begin) if stage == 0 else (total[stage - 1], at)
        index = [slice(None)] * len(left) + [slice(None), pl.ds(column, width)]
        index[place] = 1 - bit
        copy = pltpu.make_async_remote_copy(
            src_ref=ref.at[tuple(index)],
            dst_ref=got[stage].at[
                tuple([slice(None)] * (len(left) - 1) + [slice(None), pl.ds(at, width)])
            ],
            send_sem=send_sem.at[number, stage],
            recv_sem=recv_sem.at[number, stage],
            device_id=partners[path[stage]],
            device_id_type=pl.DeviceIdType.MESH,
        )
        copy.start()
        started.append(copy)
        return copy, ref, column, place, bit, len(left) - 1

    def end_stage(number, stage, state):
        copy, ref, column, place, bit, outer = state
        _, _, _, _, got, total, last, at, width, _ = pieces[number]
        copy.wait_recv()
        rows = ref.shape[-2]
        share = rows // groups
        final = stage == stages - 1
        for combo in range(2**outer):
            lead = [(combo >> (outer - 1 - n)) % 2 for n in range(outer)]
            mine = lead[:place] + [bit] + lead[place:]

            def body(r, carry):
                span = pl.ds(pl.multiple_of(r * share, share), share)
                added = ref[tuple(mine + [span, pl.ds(column, width)])].astype(
                    jnp.float32
                ) + got[stage][tuple(lead + [span, pl.ds(at, width)])].astype(jnp.float32)
                if final:
                    last[r, :, pl.ds(at, width)] = added.astype(last.dtype)
                else:
                    total[stage][tuple(lead + [span, pl.ds(at, width)])] = added.astype(
                        total[stage].dtype
                    )
                return carry

            lax.fori_loop(0, groups, body, 0)

    states = [begin_stage(number, 0) for number in range(len(pieces))]
    for stage in range(stages):
        for number in range(len(pieces)):
            end_stage(number, stage, states[number])
            if stage + 1 < stages:
                states[number] = begin_stage(number, stage + 1)
            else:
                copies = []
                _, _, _, _, got, _, last, at, width, _ = pieces[number]
                landing = rest[4 * stages + 4 + (1 if got is got_thin else 0)]
                for s, other in enumerate(others):
                    copy = pltpu.make_async_remote_copy(
                        src_ref=last.at[other, :, pl.ds(at, width)],
                        dst_ref=landing.at[s, :, pl.ds(at, width)],
                        send_sem=send_sem.at[number, stages + s],
                        recv_sem=recv_sem.at[number, stages + s],
                        device_id=(me, other),
                        device_id_type=pl.DeviceIdType.MESH,
                    )
                    copy.start()
                    started.append(copy)
                    copies.append(copy)
                states[number] = (copies, landing)
    for number in range(len(pieces)):
        copies, landing = states[number]
        _, begin, out, _, _, _, last, at, width, _ = pieces[number]
        added = last[group, :, pl.ds(at, width)].astype(jnp.float32)
        for s, copy in enumerate(copies):
            copy.wait_recv()
            added = added + landing[s, :, pl.ds(at, width)].astype(jnp.float32)
        out[:, pl.ds(begin, width)] = added
    for copy in started:
        copy.wait_send()


def sum_kernel_entry(peers, groups, wide, mid, thin, wide_out, mid_out, thin_out, *rest):
    stages = peers.bit_length() - 1
    body, (land_big, land_thin, send_sem, recv_sem) = rest[:-4], rest[-4:]
    sum_kernel(
        peers,
        groups,
        wide,
        mid,
        thin,
        wide_out,
        mid_out,
        thin_out,
        *body[: 4 * stages + 2],
        send_sem,
        recv_sem,
        land_big,
        land_thin,
    )


def summed_shares(peers, groups, wide, mid, thin):
    stages = peers.bit_length() - 1
    rows = wide.shape[0] // peers
    share = rows // groups
    columns = wide.shape[1] + mid.shape[1]
    lead = (2,) * stages
    count = columns // PIECE + 1
    last_type = jnp.bfloat16 if share % 16 == 0 else jnp.float32
    thin_columns = thin.shape[1]
    scratch = []
    for dtype, size in ((jnp.bfloat16, columns), (jnp.float32, thin_columns)):
        for _ in range(2):
            for stage in range(stages):
                scratch.append(pltpu.VMEM((2,) * (stages - 1 - stage) + (rows, size), dtype))
    scratch += [
        pltpu.VMEM((groups, share, columns), last_type),
        pltpu.VMEM((groups, share, thin_columns), jnp.float32),
        pltpu.VMEM((groups - 1, share, columns), last_type),
        pltpu.VMEM((groups - 1, share, thin_columns), jnp.float32),
        pltpu.SemaphoreType.DMA((count, stages + groups - 1)),
        pltpu.SemaphoreType.DMA((count, stages + groups - 1)),
    ]
    vmem = pl.BlockSpec(memory_space=pltpu.VMEM)
    return pl.pallas_call(
        functools.partial(sum_kernel_entry, peers, groups),
        in_specs=[vmem] * 3,
        out_specs=[vmem] * 3,
        out_shape=[
            jax.ShapeDtypeStruct((share, size), jnp.float32)
            for size in (wide.shape[1], mid.shape[1], thin_columns)
        ],
        scratch_shapes=scratch,
        compiler_params=pltpu.CompilerParams(
            collective_id=0, has_side_effects=True, vmem_limit_bytes=48 * 2**20
        ),
        name="summed_shares",
    )(
        wide.reshape(lead + (rows, wide.shape[1])),
        mid.reshape(lead + (rows, mid.shape[1])),
        thin.reshape(lead + (rows, thin_columns)),
    )


def standardise(values):
    centered = values - jnp.mean(values, axis=1, keepdims=True)
    scale = lax.rsqrt(jnp.mean(centered * centered, axis=1, keepdims=True) + EPS)
    return (centered * scale, scale)


def depth_forward(values, segment, kernel):
    width = kernel.shape[0]
    half = width // 2
    rows = values.shape[0]
    padded = jnp.pad(values, ((half, half), (0, 0)))
    labels = jnp.pad(segment, (half, half), constant_values=-1)
    total = jnp.zeros(values.shape, jnp.float32)
    for offset in range(width):
        same = labels[offset : offset + rows] == segment
        total = (
            total + jnp.where(same[:, None], padded[offset : offset + rows], 0.0) * kernel[offset]
        )
    return total


def depth_backward(values, grad_depth, segment, kernel):
    width = kernel.shape[0]
    half = width // 2
    rows = values.shape[0]
    padded = jnp.pad(values, ((half, half), (0, 0)))
    padded_grad = jnp.pad(grad_depth, ((half, half), (0, 0)))
    labels = jnp.pad(segment, (half, half), constant_values=-1)
    grad_in = jnp.zeros(values.shape, jnp.float32)
    kernel_rows = []
    for offset in range(width):
        same = labels[offset : offset + rows] == segment
        shifted = jnp.where(same[:, None], padded[offset : offset + rows], 0.0)
        kernel_rows.append(jnp.sum(shifted * grad_depth, axis=0))
        back = 2 * half - offset
        same_back = labels[back : back + rows] == segment
        grad_in = (
            grad_in
            + jnp.where(same_back[:, None], padded_grad[back : back + rows], 0.0) * kernel[offset]
        )
    return (grad_in, jnp.stack(kernel_rows, axis=0))


def module(
    hidden_in,
    row_mask,
    segment,
    cotangent,
    pre_gain,
    expand_weight,
    depth_kernel,
    mid_gain,
    output_weight,
    settle,
):
    width = hidden_in.shape[1]
    hidden = hidden_in.astype(jnp.float32)
    normed_in = standardise(hidden)[0]
    norm_in = (normed_in * pre_gain).astype(jnp.bfloat16)
    expanded = product(norm_in, expand_weight)
    value = expanded[:, :width]
    gate = jax.nn.sigmoid(expanded[:, width:])
    gated = value * gate * row_mask[:, None]
    depth_out = depth_forward(gated, segment, depth_kernel)
    normed_mid, scale_mid = standardise(depth_out)
    scaled_mid = normed_mid * mid_gain
    sigma = jax.nn.sigmoid(scaled_mid)
    swish = (scaled_mid * sigma).astype(jnp.bfloat16)
    encoded = ((hidden + product(swish, output_weight)) * row_mask[:, None]).astype(jnp.bfloat16)
    grad_out = jnp.where(row_mask[:, None] > 0, cotangent, jnp.zeros((), cotangent.dtype))
    output_grad = over_rows(swish, grad_out)
    grad_swish = against(grad_out, output_weight)
    grad_scaled = grad_swish * (sigma + scaled_mid * sigma * (1.0 - sigma))
    midnorm_grad = jnp.sum(grad_scaled * normed_mid, axis=0)
    settled = settle(output_grad, midnorm_grad)
    excess = grad_scaled * mid_gain
    grad_depth = scale_mid * (
        excess
        - jnp.mean(excess, axis=1, keepdims=True)
        - normed_mid * jnp.mean(excess * normed_mid, axis=1, keepdims=True)
    )
    grad_gated, kernel_grad = depth_backward(gated, grad_depth, segment, depth_kernel)
    grad_gated = grad_gated * row_mask[:, None]
    grad_expanded = jnp.concatenate(
        [grad_gated * gate, grad_gated * value * gate * (1.0 - gate)], axis=1
    ).astype(jnp.bfloat16)
    expand_grad = over_rows(norm_in, grad_expanded)
    grad_norm = against(grad_expanded, expand_weight)
    prenorm_grad = jnp.sum(grad_norm * normed_in, axis=0)
    return (encoded, (expand_grad, kernel_grad, prenorm_grad), settled)


def per_device(
    frames,
    lengths,
    targets,
    offsets,
    first_filter,
    second_filter,
    projection,
    pre_gain,
    expand_weight,
    depth_kernel,
    mid_gain,
    output_weight,
    cotangent,
):
    peers = lax.axis_size("dp")
    stored = frames[0]
    sizes = lengths[0]
    routes = targets[0]
    starts_at = offsets[0]
    blocks_used = (sizes + FB - 1) // FB
    first_stored = jnp.cumsum(blocks_used) - blocks_used
    match = ((routes[:, None] == jnp.arange(peers)[None, :]) & (sizes[:, None] > 0)).astype(
        jnp.int32
    )
    send_blocks = jnp.sum(match * blocks_used[:, None], axis=0)
    send_first = jnp.sum(match * first_stored[:, None], axis=0)
    send_offset = jnp.sum(match * starts_at[:, None], axis=0)
    send_length = jnp.sum(match * sizes[:, None], axis=0)
    within = jnp.arange(CAP)
    used = within[None, :] < send_blocks[:, None]
    source_rows = jnp.clip(send_first[:, None] + within[None, :], 0, stored.shape[0] - 1)
    outgoing = jnp.take(stored, source_rows.reshape(-1), axis=0).reshape(
        peers, CAP, stored.shape[1]
    )
    labels = jnp.stack(
        [
            jnp.where(used, send_offset[:, None] + within[None, :], -1),
            jnp.where(used, jnp.clip(send_length[:, None] - within[None, :] * FB, 0, FB), 0),
            jnp.broadcast_to(send_offset[:, None], (peers, CAP)),
        ],
        axis=2,
    )
    incoming, arrived = (
        lax.all_to_all(outgoing, "dp", split_axis=0, concat_axis=0, tiled=True),
        lax.all_to_all(labels, "dp", split_axis=0, concat_axis=0, tiled=True),
    )
    received = incoming.reshape(peers * CAP, stored.shape[1])
    tags = arrived.reshape(peers * CAP, 3)
    placing = tags[None, :, 0] == jnp.arange(R_DEV)[:, None]
    blocks = jnp.dot(
        placing.astype(jnp.bfloat16), received, preferred_element_type=jnp.float32
    ).astype(jnp.bfloat16)
    placing_count = placing.astype(jnp.int32)
    valid_frames = jnp.sum(placing_count * tags[None, :, 1], axis=1)
    first_slot = jnp.sum(placing_count * tags[None, :, 2], axis=1)
    is_first = first_slot == jnp.arange(R_DEV)
    features, row_mask = subsample(blocks, valid_frames, is_first, first_filter, second_filter)
    projected = jnp.dot(
        features,
        lax.all_gather(projection, ("dp", "group"), axis=0, tiled=True),
        preferred_element_type=jnp.float32,
    )
    hidden_in = projected.astype(jnp.bfloat16)
    hidden_in = hidden_in.reshape(FS, R_DEV, -1).transpose(1, 0, 2).reshape(hidden_in.shape)
    segment = jnp.repeat(first_slot, FS)

    def settle(output_term, midnorm_term):
        return (output_term, midnorm_term)

    encoded, rest, settled = module(
        hidden_in,
        row_mask,
        segment,
        cotangent[0],
        pre_gain,
        expand_weight,
        depth_kernel,
        mid_gain,
        output_weight,
        settle,
    )
    taps = rest[1].shape[0]
    thin = jnp.concatenate([rest[1], rest[2][None], settled[1][None]], axis=0)
    thin = jnp.pad(thin, ((0, LANES - taps - 2), (0, 0))).T
    wide, mid, thin = summed_shares(
        peers,
        lax.axis_size("group"),
        rest[0].astype(jnp.bfloat16),
        settled[0].astype(jnp.bfloat16),
        thin,
    )
    small = thin.T
    return (encoded[None], wide, mid, small[:taps], small[taps], small[taps + 1])


def solution(mesh):
    return jax.shard_map(
        per_device,
        mesh=mesh,
        in_specs=(
            P("group", "dp", None),
            P("group", "dp"),
            P("group", "dp"),
            P("group", "dp"),
            P(),
            P(),
            P(("dp", "group"), None),
            P(),
            P(),
            P(),
            P(),
            P(),
            P("group", "dp", None),
        ),
        out_specs=(
            P("group", "dp", None),
            P(("dp", "group"), None),
            P(("dp", "group"), None),
            P(None, ("dp", "group")),
            P(("dp", "group")),
            P(("dp", "group")),
        ),
        check_vma=False,
    )
```

```python
import functools

import jax
import jax.numpy as jnp
from jax import lax
from jax.experimental import pallas as pl
from jax.experimental.pallas import tpu as pltpu
from jax.sharding import PartitionSpec as P

MEL = 80
FB = 48
CAP = 3
R_DEV = 16
FS = 12


EPS = 1e-05


def product(left, right):
    return jnp.dot(left, right, preferred_element_type=jnp.float32)


def over_rows(left, right):
    return lax.dot_general(
        left, right, (((0,), (0,)), ((), ())), preferred_element_type=jnp.float32
    )


def against(left, right):
    return lax.dot_general(
        left, right, (((1,), (1,)), ((), ())), preferred_element_type=jnp.float32
    )


FC = 5
LANES = 128


def conv_kernel(width, blocks_ref, valid_ref, first_ref, one_ref, two_ref, out_ref, taps, keep, even, odd):
    step = pl.program_id(0)
    slots = blocks_ref.shape[0]
    rows = slots * FS
    channels = two_ref.shape[2]

    @pl.when(step == 0)
    def _():
        valid = valid_ref[...]
        later = first_ref[...] == 0
        lane = lax.broadcasted_iota(jnp.int32, (slots, 2 * LANES), 1)
        inside = (lane >= 1) & (lane <= MEL)
        pieces = []
        for k in range(FB):
            start = MEL * k
            base = start // LANES * LANES
            if base + 2 * LANES <= FB * MEL:
                window = blocks_ref[:, base : base + 2 * LANES].astype(jnp.float32)
            else:
                tail = blocks_ref[:, base : base + LANES].astype(jnp.float32)
                window = jnp.concatenate([tail, jnp.zeros_like(tail)], axis=1)
            moved = pltpu.roll(window, (1 - (start - base)) % (2 * LANES), 1)
            moved = jnp.where(inside, moved, 0.0)[:, :LANES]
            pieces.append(jnp.where(k < valid, moved, 0.0))
        before = {}
        for back in (1, 2, 3):
            before[-back] = jnp.where(later, pltpu.roll(pieces[FB - back], 1, 0), 0.0)

        def frame(k):
            return before[k] if k < 0 else pieces[k]

        last_valid = pltpu.roll(valid.astype(jnp.float32), 1, 0)
        for kk in range(FS):
            for part, offset in ((0, -3), (1, -1), (2, 1)):
                at = part * rows + kk * slots
                for i in range(3):
                    taps[at : at + slots, i * LANES : (i + 1) * LANES] = frame(
                        4 * kk + offset + i
                    ).astype(jnp.bfloat16)
                if part == 0 and kk == 0:
                    kept = (last_valid > FB - 2.0) & later
                else:
                    kept = 4 * kk + 2 * (part - 1) < valid
                keep[at : at + slots, :] = kept.astype(jnp.float32)
        odd[:, 0] = jnp.zeros(odd.shape[:1] + odd.shape[2:], odd.dtype)

    @pl.when(step > 0)
    def _():
        odd[:, 0] = odd[:, FC]

    picked = lax.broadcasted_iota(jnp.int32, (3 * LANES, LANES), 0)
    column = lax.broadcasted_iota(jnp.int32, (3 * LANES, LANES), 1)
    wanted = jnp.full((3 * LANES, LANES), -4 * MEL, jnp.int32)
    for i in range(3):
        wanted = jnp.where(
            (column >= 5 * i) & (column < 5 * i + 5), i * LANES + column - 5 * i, wanted
        )
    for local in range(FC):
        shift = 4 * (step * FC + local)
        chosen = jnp.where(picked == wanted + shift, 1.0, 0.0).astype(jnp.bfloat16)
        for part in range(3):
            span = slice(part * rows, (part + 1) * rows)
            window = product(taps[span, :], chosen).astype(jnp.bfloat16)
            mask = keep[span, 0:1] > 0
            level = jnp.where(mask, jnp.maximum(product(window, one_ref[...]), 0.0), 0.0).astype(
                jnp.bfloat16
            )
            even[part, local] = level[:, :channels]
            odd[part, local + 1] = level[:, channels:]
    total = jnp.zeros((FC * rows, channels), jnp.float32)
    for i in range(3):
        for j, source in ((0, odd[i, 0:FC]), (1, even[i]), (2, odd[i, 1 : FC + 1])):
            total = total + product(source.reshape(FC * rows, channels), two_ref[3 * i + j])
    mask = keep[rows : 2 * rows, 0:1] > 0
    block = width
    for local in range(FC):
        part = total[local * rows : (local + 1) * rows]
        part = jnp.where(mask, jnp.maximum(part, 0.0), 0.0).astype(jnp.bfloat16)
        at = local * channels
        while at < (local + 1) * channels:
            number = at // block
            end = min((number + 1) * block, (local + 1) * channels)
            to = number // 2 * block + at - number * block
            out_ref[number % 2, :, to : to + end - at] = part[
                :, at - local * channels : end - local * channels
            ]
            at = end


def subsample(blocks, valid_frames, is_first, first_filter, second_filter, width):
    slots = blocks.shape[0]
    channels = first_filter.shape[2]
    rows = slots * FS
    bins = MEL // 4
    low = jnp.pad(first_filter, ((0, 0), (0, 2), (0, 0)))
    high = jnp.pad(first_filter, ((0, 0), (2, 0), (0, 0)))
    one = jnp.concatenate([low, high], axis=2).reshape(15, 2 * channels)
    one = jnp.pad(one, ((0, LANES - 15), (0, 0)))
    two = second_filter.reshape(9, channels, channels)
    valid = jnp.broadcast_to(valid_frames[:, None], (slots, LANES))
    first = jnp.broadcast_to(is_first[:, None], (slots, LANES)).astype(jnp.int32)
    whole = lambda shape: pl.BlockSpec(shape, lambda s: (0,) * len(shape))
    features = pl.pallas_call(
        functools.partial(conv_kernel, width),
        grid=(bins // FC,),
        in_specs=[
            whole(blocks.shape),
            whole(valid.shape),
            whole(first.shape),
            whole(one.shape),
            whole(two.shape),
        ],
        out_specs=pl.BlockSpec((2, rows, FC * channels // 2), lambda s: (0, 0, s)),
        out_shape=jax.ShapeDtypeStruct((2, rows, bins * channels // 2), jnp.bfloat16),
        scratch_shapes=[
            pltpu.VMEM((3 * rows, 3 * LANES), jnp.bfloat16),
            pltpu.VMEM((3 * rows, LANES), jnp.float32),
            pltpu.VMEM((3, FC, rows, channels), jnp.bfloat16),
            pltpu.VMEM((3, FC + 1, rows, channels), jnp.bfloat16),
        ],
        compiler_params=pltpu.CompilerParams(vmem_limit_bytes=44 * 2**20),
        cost_estimate=pl.CostEstimate(
            flops=30 * 10**9, bytes_accessed=10 * 2**20, transcendentals=0
        ),
        name="subsample",
    )(blocks, valid, first, one, two)
    keep_two = 4 * jnp.arange(FS)[None, :] < valid_frames[:, None]
    return (features, keep_two.reshape(-1).astype(jnp.float32))


PIECE = 512


def sum_kernel(peers, groups, wide_ref, mid_ref, thin_ref, wide_out, mid_out, thin_out, *rest):
    stages = peers.bit_length() - 1
    got_big = rest[:stages]
    sum_big = rest[stages : 2 * stages]
    got_thin = rest[2 * stages : 3 * stages]
    sum_thin = rest[3 * stages : 4 * stages]
    last_big, last_thin, send_sem, recv_sem = rest[4 * stages : 4 * stages + 4]
    me = lax.axis_index("dp")
    group = lax.axis_index("group")
    bits = [(me // 2**b) % 2 for b in range(stages)]
    partners = [(me + (1 - 2 * bits[b]) * 2**b, group) for b in range(stages)]
    others = [lax.rem(group + s, groups) for s in range(1, groups)]
    barrier = pltpu.get_barrier_semaphore()
    for device in partners + [(me, other) for other in others]:
        pl.semaphore_signal(
            barrier, inc=1, device_id=device, device_id_type=pl.DeviceIdType.MESH
        )
    pl.semaphore_wait(barrier, stages + groups - 1)

    pieces = []
    order = [0] + list(range(1, stages))
    swapped = [0] + list(range(stages - 1, 0, -1))
    at = 0
    for source, out in ((wide_ref, wide_out), (mid_ref, mid_out)):
        for begin in range(0, source.shape[-1], PIECE):
            path = order if len(pieces) % 2 == 0 else swapped
            pieces.append((source, begin, out, begin, got_big, sum_big, last_big, at, PIECE, path))
            at += PIECE
    pieces.append(
        (thin_ref, 0, thin_out, 0, got_thin, sum_thin, last_thin, 0, thin_ref.shape[-1], order)
    )
    pieces = pieces[-1:] + pieces[:-1]
    started = []

    def begin_stage(number, stage):
        source, begin, _, _, got, total, _, at, width, path = pieces[number]
        left = [b for b in range(stages - 1, -1, -1) if b not in path[:stage]]
        place = left.index(path[stage])
        bit = bits[path[stage]]
        ref, column = (source, begin) if stage == 0 else (total[stage - 1], at)
        index = [slice(None)] * len(left) + [slice(None), pl.ds(column, width)]
        index[place] = 1 - bit
        copy = pltpu.make_async_remote_copy(
            src_ref=ref.at[tuple(index)],
            dst_ref=got[stage].at[
                tuple([slice(None)] * (len(left) - 1) + [slice(None), pl.ds(at, width)])
            ],
            send_sem=send_sem.at[number, stage],
            recv_sem=recv_sem.at[number, stage],
            device_id=partners[path[stage]],
            device_id_type=pl.DeviceIdType.MESH,
        )
        copy.start()
        started.append(copy)
        return copy, ref, column, place, bit, len(left) - 1

    def end_stage(number, stage, state):
        copy, ref, column, place, bit, outer = state
        _, _, _, _, got, total, last, at, width, _ = pieces[number]
        copy.wait_recv()
        rows = ref.shape[-2]
        share = rows // groups
        final = stage == stages - 1
        for combo in range(2**outer):
            lead = [(combo >> (outer - 1 - n)) % 2 for n in range(outer)]
            mine = lead[:place] + [bit] + lead[place:]

            def body(r, carry):
                span = pl.ds(pl.multiple_of(r * share, share), share)
                added = ref[tuple(mine + [span, pl.ds(column, width)])].astype(
                    jnp.float32
                ) + got[stage][tuple(lead + [span, pl.ds(at, width)])].astype(jnp.float32)
                if final:
                    last[r, :, pl.ds(at, width)] = added.astype(last.dtype)
                else:
                    total[stage][tuple(lead + [span, pl.ds(at, width)])] = added.astype(
                        total[stage].dtype
                    )
                return carry

            lax.fori_loop(0, groups, body, 0)

    states = [begin_stage(number, 0) for number in range(len(pieces))]
    for stage in range(stages):
        for number in range(len(pieces)):
            end_stage(number, stage, states[number])
            if stage + 1 < stages:
                states[number] = begin_stage(number, stage + 1)
            else:
                copies = []
                _, _, _, _, got, _, last, at, width, _ = pieces[number]
                landing = rest[4 * stages + 4 + (1 if got is got_thin else 0)]
                for s, other in enumerate(others):
                    copy = pltpu.make_async_remote_copy(
                        src_ref=last.at[other, :, pl.ds(at, width)],
                        dst_ref=landing.at[s, :, pl.ds(at, width)],
                        send_sem=send_sem.at[number, stages + s],
                        recv_sem=recv_sem.at[number, stages + s],
                        device_id=(me, other),
                        device_id_type=pl.DeviceIdType.MESH,
                    )
                    copy.start()
                    started.append(copy)
                    copies.append(copy)
                states[number] = (copies, landing)
    for number in range(len(pieces)):
        copies, landing = states[number]
        _, begin, out, _, _, _, last, at, width, _ = pieces[number]
        added = last[group, :, pl.ds(at, width)].astype(jnp.float32)
        for s, copy in enumerate(copies):
            copy.wait_recv()
            added = added + landing[s, :, pl.ds(at, width)].astype(jnp.float32)
        out[:, pl.ds(begin, width)] = added
    for copy in started:
        copy.wait_send()


def sum_kernel_entry(peers, groups, wide, mid, thin, wide_out, mid_out, thin_out, *rest):
    stages = peers.bit_length() - 1
    body, (land_big, land_thin, send_sem, recv_sem) = rest[:-4], rest[-4:]
    sum_kernel(
        peers,
        groups,
        wide,
        mid,
        thin,
        wide_out,
        mid_out,
        thin_out,
        *body[: 4 * stages + 2],
        send_sem,
        recv_sem,
        land_big,
        land_thin,
    )


def summed_shares(peers, groups, wide, mid, thin):
    stages = peers.bit_length() - 1
    rows = wide.shape[0] // peers
    share = rows // groups
    columns = wide.shape[1] + mid.shape[1]
    lead = (2,) * stages
    count = columns // PIECE + 1
    last_type = jnp.bfloat16 if share % 16 == 0 else jnp.float32
    thin_columns = thin.shape[1]
    scratch = []
    for dtype, size in ((jnp.bfloat16, columns), (jnp.float32, thin_columns)):
        for _ in range(2):
            for stage in range(stages):
                scratch.append(pltpu.VMEM((2,) * (stages - 1 - stage) + (rows, size), dtype))
    scratch += [
        pltpu.VMEM((groups, share, columns), last_type),
        pltpu.VMEM((groups, share, thin_columns), jnp.float32),
        pltpu.VMEM((groups - 1, share, columns), last_type),
        pltpu.VMEM((groups - 1, share, thin_columns), jnp.float32),
        pltpu.SemaphoreType.DMA((count, stages + groups - 1)),
        pltpu.SemaphoreType.DMA((count, stages + groups - 1)),
    ]
    vmem = pl.BlockSpec(memory_space=pltpu.VMEM)
    return pl.pallas_call(
        functools.partial(sum_kernel_entry, peers, groups),
        in_specs=[vmem] * 3,
        out_specs=[vmem] * 3,
        out_shape=[
            jax.ShapeDtypeStruct((share, size), jnp.float32)
            for size in (wide.shape[1], mid.shape[1], thin_columns)
        ],
        scratch_shapes=scratch,
        compiler_params=pltpu.CompilerParams(
            collective_id=0, has_side_effects=True, vmem_limit_bytes=48 * 2**20
        ),
        name="summed_shares",
    )(
        wide.reshape(lead + (rows, wide.shape[1])),
        mid.reshape(lead + (rows, mid.shape[1])),
        thin.reshape(lead + (rows, thin_columns)),
    )


def standardise(values):
    centered = values - jnp.mean(values, axis=1, keepdims=True)
    scale = lax.rsqrt(jnp.mean(centered * centered, axis=1, keepdims=True) + EPS)
    return (centered * scale, scale)


def depth_forward(values, segment, kernel):
    width = kernel.shape[0]
    half = width // 2
    rows = values.shape[0]
    padded = jnp.pad(values, ((half, half), (0, 0)))
    labels = jnp.pad(segment, (half, half), constant_values=-1)
    total = jnp.zeros(values.shape, jnp.float32)
    for offset in range(width):
        same = labels[offset : offset + rows] == segment
        total = (
            total + jnp.where(same[:, None], padded[offset : offset + rows], 0.0) * kernel[offset]
        )
    return total


def depth_backward(values, grad_depth, segment, kernel):
    width = kernel.shape[0]
    half = width // 2
    rows = values.shape[0]
    padded = jnp.pad(values, ((half, half), (0, 0)))
    padded_grad = jnp.pad(grad_depth, ((half, half), (0, 0)))
    labels = jnp.pad(segment, (half, half), constant_values=-1)
    grad_in = jnp.zeros(values.shape, jnp.float32)
    kernel_rows = []
    for offset in range(width):
        same = labels[offset : offset + rows] == segment
        shifted = jnp.where(same[:, None], padded[offset : offset + rows], 0.0)
        kernel_rows.append(jnp.sum(shifted * grad_depth, axis=0))
        back = 2 * half - offset
        same_back = labels[back : back + rows] == segment
        grad_in = (
            grad_in
            + jnp.where(same_back[:, None], padded_grad[back : back + rows], 0.0) * kernel[offset]
        )
    return (grad_in, jnp.stack(kernel_rows, axis=0))


def module(
    hidden_in,
    row_mask,
    segment,
    cotangent,
    pre_gain,
    expand_weight,
    depth_kernel,
    mid_gain,
    output_weight,
    settle,
):
    width = hidden_in.shape[1]
    hidden = hidden_in.astype(jnp.float32)
    normed_in = standardise(hidden)[0]
    norm_in = (normed_in * pre_gain).astype(jnp.bfloat16)
    expanded = product(norm_in, expand_weight)
    value = expanded[:, :width]
    gate = jax.nn.sigmoid(expanded[:, width:])
    gated = value * gate * row_mask[:, None]
    depth_out = depth_forward(gated, segment, depth_kernel)
    normed_mid, scale_mid = standardise(depth_out)
    scaled_mid = normed_mid * mid_gain
    sigma = jax.nn.sigmoid(scaled_mid)
    swish = (scaled_mid * sigma).astype(jnp.bfloat16)
    encoded = ((hidden + product(swish, output_weight)) * row_mask[:, None]).astype(jnp.bfloat16)
    grad_out = jnp.where(row_mask[:, None] > 0, cotangent, jnp.zeros((), cotangent.dtype))
    output_grad = over_rows(swish, grad_out)
    grad_swish = against(grad_out, output_weight)
    grad_scaled = grad_swish * (sigma + scaled_mid * sigma * (1.0 - sigma))
    midnorm_grad = jnp.sum(grad_scaled * normed_mid, axis=0)
    settled = settle(output_grad, midnorm_grad)
    excess = grad_scaled * mid_gain
    grad_depth = scale_mid * (
        excess
        - jnp.mean(excess, axis=1, keepdims=True)
        - normed_mid * jnp.mean(excess * normed_mid, axis=1, keepdims=True)
    )
    grad_gated, kernel_grad = depth_backward(gated, grad_depth, segment, depth_kernel)
    grad_gated = grad_gated * row_mask[:, None]
    grad_expanded = jnp.concatenate(
        [grad_gated * gate, grad_gated * value * gate * (1.0 - gate)], axis=1
    ).astype(jnp.bfloat16)
    expand_grad = over_rows(norm_in, grad_expanded)
    grad_norm = against(grad_expanded, expand_weight)
    prenorm_grad = jnp.sum(grad_norm * normed_in, axis=0)
    return (encoded, (expand_grad, kernel_grad, prenorm_grad), settled)


def per_device(
    frames,
    lengths,
    targets,
    offsets,
    first_filter,
    second_filter,
    projection,
    pre_gain,
    expand_weight,
    depth_kernel,
    mid_gain,
    output_weight,
    cotangent,
):
    peers = lax.axis_size("dp")
    stored = frames[0]
    sizes = lengths[0]
    routes = targets[0]
    starts_at = offsets[0]
    blocks_used = (sizes + FB - 1) // FB
    first_stored = jnp.cumsum(blocks_used) - blocks_used
    match = ((routes[:, None] == jnp.arange(peers)[None, :]) & (sizes[:, None] > 0)).astype(
        jnp.int32
    )
    send_blocks = jnp.sum(match * blocks_used[:, None], axis=0)
    send_first = jnp.sum(match * first_stored[:, None], axis=0)
    send_offset = jnp.sum(match * starts_at[:, None], axis=0)
    send_length = jnp.sum(match * sizes[:, None], axis=0)
    within = jnp.arange(CAP)
    used = within[None, :] < send_blocks[:, None]
    source_rows = jnp.clip(send_first[:, None] + within[None, :], 0, stored.shape[0] - 1)
    outgoing = jnp.take(stored, source_rows.reshape(-1), axis=0).reshape(
        peers, CAP, stored.shape[1]
    )
    labels = jnp.stack(
        [
            jnp.where(used, send_offset[:, None] + within[None, :], -1),
            jnp.where(used, jnp.clip(send_length[:, None] - within[None, :] * FB, 0, FB), 0),
            jnp.broadcast_to(send_offset[:, None], (peers, CAP)),
        ],
        axis=2,
    )
    incoming, arrived = (
        lax.all_to_all(outgoing, "dp", split_axis=0, concat_axis=0, tiled=True),
        lax.all_to_all(labels, "dp", split_axis=0, concat_axis=0, tiled=True),
    )
    received = incoming.reshape(peers * CAP, stored.shape[1])
    tags = arrived.reshape(peers * CAP, 3)
    placing = tags[None, :, 0] == jnp.arange(R_DEV)[:, None]
    blocks = jnp.dot(
        placing.astype(jnp.bfloat16), received, preferred_element_type=jnp.float32
    ).astype(jnp.bfloat16)
    placing_count = placing.astype(jnp.int32)
    valid_frames = jnp.sum(placing_count * tags[None, :, 1], axis=1)
    first_slot = jnp.sum(placing_count * tags[None, :, 2], axis=1)
    is_first = first_slot == jnp.arange(R_DEV)
    groups = lax.axis_size("group")
    width = projection.shape[0] * groups
    features, row_mask = subsample(
        blocks, valid_frames, is_first, first_filter, second_filter, width
    )
    members = [
        [p * groups + g for p in range(c, peers, 2) for g in range(groups)] for c in range(2)
    ]
    half_weight = lax.all_gather(
        projection, ("dp", "group"), axis=0, tiled=True, axis_index_groups=members
    )
    side = lax.axis_index("dp") % 2
    swap = [(p, p ^ 1) for p in range(peers)]
    mine = lax.dynamic_index_in_dim(features, side, 0, keepdims=False)
    theirs = lax.dynamic_index_in_dim(features, 1 - side, 0, keepdims=False)
    theirs = lax.ppermute(theirs, "dp", swap)
    kept = product(mine, half_weight)
    sent = lax.ppermute(product(theirs, half_weight), "dp", swap)
    hidden_in = (kept + sent).astype(jnp.bfloat16)
    hidden_in = hidden_in.reshape(FS, R_DEV, -1).transpose(1, 0, 2).reshape(hidden_in.shape)
    segment = jnp.repeat(first_slot, FS)

    def settle(output_term, midnorm_term):
        return (output_term, midnorm_term)

    encoded, rest, settled = module(
        hidden_in,
        row_mask,
        segment,
        cotangent[0],
        pre_gain,
        expand_weight,
        depth_kernel,
        mid_gain,
        output_weight,
        settle,
    )
    taps = rest[1].shape[0]
    thin = jnp.concatenate([rest[1], rest[2][None], settled[1][None]], axis=0)
    thin = jnp.pad(thin, ((0, LANES - taps - 2), (0, 0))).T
    wide, mid, thin = summed_shares(
        peers,
        lax.axis_size("group"),
        rest[0].astype(jnp.bfloat16),
        settled[0].astype(jnp.bfloat16),
        thin,
    )
    small = thin.T
    return (encoded[None], wide, mid, small[:taps], small[taps], small[taps + 1])


def solution(mesh):
    return jax.shard_map(
        per_device,
        mesh=mesh,
        in_specs=(
            P("group", "dp", None),
            P("group", "dp"),
            P("group", "dp"),
            P("group", "dp"),
            P(),
            P(),
            P(("dp", "group"), None),
            P(),
            P(),
            P(),
            P(),
            P(),
            P("group", "dp", None),
        ),
        out_specs=(
            P("group", "dp", None),
            P(("dp", "group"), None),
            P(("dp", "group"), None),
            P(None, ("dp", "group")),
            P(("dp", "group")),
            P(("dp", "group")),
        ),
        check_vma=False,
    )
```

```python
import functools

import jax
import jax.numpy as jnp
from jax import lax
from jax.experimental import pallas as pl
from jax.experimental.pallas import tpu as pltpu
from jax.sharding import PartitionSpec as P

MEL = 80
FB = 48
CAP = 3
R_DEV = 16
FS = 12


EPS = 1e-05


def product(left, right):
    return jnp.dot(left, right, preferred_element_type=jnp.float32)


def over_rows(left, right):
    return lax.dot_general(
        left, right, (((0,), (0,)), ((), ())), preferred_element_type=jnp.float32
    )


def against(left, right):
    return lax.dot_general(
        left, right, (((1,), (1,)), ((), ())), preferred_element_type=jnp.float32
    )


FC = 5
LANES = 128


def conv_kernel(width, blocks_ref, valid_ref, first_ref, one_ref, two_ref, out_ref, taps, keep, even, odd):
    step = pl.program_id(0)
    slots = blocks_ref.shape[0]
    rows = slots * FS
    channels = two_ref.shape[2]

    @pl.when(step == 0)
    def _():
        valid = valid_ref[...]
        later = first_ref[...] == 0
        lane = lax.broadcasted_iota(jnp.int32, (slots, 2 * LANES), 1)
        inside = (lane >= 1) & (lane <= MEL)
        pieces = []
        for k in range(FB):
            start = MEL * k
            base = start // LANES * LANES
            if base + 2 * LANES <= FB * MEL:
                window = blocks_ref[:, base : base + 2 * LANES].astype(jnp.float32)
            else:
                tail = blocks_ref[:, base : base + LANES].astype(jnp.float32)
                window = jnp.concatenate([tail, jnp.zeros_like(tail)], axis=1)
            moved = pltpu.roll(window, (1 - (start - base)) % (2 * LANES), 1)
            moved = jnp.where(inside, moved, 0.0)[:, :LANES]
            pieces.append(jnp.where(k < valid, moved, 0.0))
        before = {}
        for back in (1, 2, 3):
            before[-back] = jnp.where(later, pltpu.roll(pieces[FB - back], 1, 0), 0.0)

        def frame(k):
            return before[k] if k < 0 else pieces[k]

        last_valid = pltpu.roll(valid.astype(jnp.float32), 1, 0)
        for kk in range(FS):
            for part, offset in ((0, -3), (1, -1), (2, 1)):
                at = part * rows + kk * slots
                for i in range(3):
                    taps[at : at + slots, i * LANES : (i + 1) * LANES] = frame(
                        4 * kk + offset + i
                    ).astype(jnp.bfloat16)
                if part == 0 and kk == 0:
                    kept = (last_valid > FB - 2.0) & later
                else:
                    kept = 4 * kk + 2 * (part - 1) < valid
                keep[at : at + slots, :] = kept.astype(jnp.float32)
        odd[:, 0] = jnp.zeros(odd.shape[:1] + odd.shape[2:], odd.dtype)

    @pl.when(step > 0)
    def _():
        odd[:, 0] = odd[:, FC]

    picked = lax.broadcasted_iota(jnp.int32, (3 * LANES, LANES), 0)
    column = lax.broadcasted_iota(jnp.int32, (3 * LANES, LANES), 1)
    wanted = jnp.full((3 * LANES, LANES), -4 * MEL, jnp.int32)
    for i in range(3):
        wanted = jnp.where(
            (column >= 5 * i) & (column < 5 * i + 5), i * LANES + column - 5 * i, wanted
        )
    for local in range(FC):
        shift = 4 * (step * FC + local)
        chosen = jnp.where(picked == wanted + shift, 1.0, 0.0).astype(jnp.bfloat16)
        for part in range(3):
            span = slice(part * rows, (part + 1) * rows)
            window = product(taps[span, :], chosen).astype(jnp.bfloat16)
            mask = keep[span, 0:1] > 0
            level = jnp.where(mask, jnp.maximum(product(window, one_ref[...]), 0.0), 0.0).astype(
                jnp.bfloat16
            )
            even[part, local] = level[:, :channels]
            odd[part, local + 1] = level[:, channels:]
    total = jnp.zeros((FC * rows, channels), jnp.float32)
    for i in range(3):
        for j, source in ((0, odd[i, 0:FC]), (1, even[i]), (2, odd[i, 1 : FC + 1])):
            total = total + product(source.reshape(FC * rows, channels), two_ref[3 * i + j])
    mask = keep[rows : 2 * rows, 0:1] > 0
    block = width
    for local in range(FC):
        part = total[local * rows : (local + 1) * rows]
        part = jnp.where(mask, jnp.maximum(part, 0.0), 0.0).astype(jnp.bfloat16)
        at = local * channels
        while at < (local + 1) * channels:
            number = at // block
            end = min((number + 1) * block, (local + 1) * channels)
            to = number // 2 * block + at - number * block
            out_ref[number % 2, :, to : to + end - at] = part[
                :, at - local * channels : end - local * channels
            ]
            at = end


def subsample(blocks, valid_frames, is_first, first_filter, second_filter, width):
    slots = blocks.shape[0]
    channels = first_filter.shape[2]
    rows = slots * FS
    bins = MEL // 4
    low = jnp.pad(first_filter, ((0, 0), (0, 2), (0, 0)))
    high = jnp.pad(first_filter, ((0, 0), (2, 0), (0, 0)))
    one = jnp.concatenate([low, high], axis=2).reshape(15, 2 * channels)
    one = jnp.pad(one, ((0, LANES - 15), (0, 0)))
    two = second_filter.reshape(9, channels, channels)
    valid = jnp.broadcast_to(valid_frames[:, None], (slots, LANES))
    first = jnp.broadcast_to(is_first[:, None], (slots, LANES)).astype(jnp.int32)
    whole = lambda shape: pl.BlockSpec(shape, lambda s: (0,) * len(shape))
    features = pl.pallas_call(
        functools.partial(conv_kernel, width),
        grid=(bins // FC,),
        in_specs=[
            whole(blocks.shape),
            whole(valid.shape),
            whole(first.shape),
            whole(one.shape),
            whole(two.shape),
        ],
        out_specs=pl.BlockSpec((2, rows, FC * channels // 2), lambda s: (0, 0, s)),
        out_shape=jax.ShapeDtypeStruct((2, rows, bins * channels // 2), jnp.bfloat16),
        scratch_shapes=[
            pltpu.VMEM((3 * rows, 3 * LANES), jnp.bfloat16),
            pltpu.VMEM((3 * rows, LANES), jnp.float32),
            pltpu.VMEM((3, FC, rows, channels), jnp.bfloat16),
            pltpu.VMEM((3, FC + 1, rows, channels), jnp.bfloat16),
        ],
        compiler_params=pltpu.CompilerParams(vmem_limit_bytes=44 * 2**20),
        cost_estimate=pl.CostEstimate(
            flops=30 * 10**9, bytes_accessed=10 * 2**20, transcendentals=0
        ),
        name="subsample",
    )(blocks, valid, first, one, two)
    keep_two = 4 * jnp.arange(FS)[None, :] < valid_frames[:, None]
    return (features, keep_two.reshape(-1).astype(jnp.float32))


PIECE = 512


def sum_kernel(peers, groups, wide_ref, mid_ref, thin_ref, wide_out, mid_out, thin_out, *rest):
    stages = peers.bit_length() - 1
    got_big = rest[:stages]
    sum_big = rest[stages : 2 * stages]
    got_thin = rest[2 * stages : 3 * stages]
    sum_thin = rest[3 * stages : 4 * stages]
    last_big, last_thin, send_sem, recv_sem = rest[4 * stages : 4 * stages + 4]
    me = lax.axis_index("dp")
    group = lax.axis_index("group")
    bits = [(me // 2**b) % 2 for b in range(stages)]
    partners = [(me + (1 - 2 * bits[b]) * 2**b, group) for b in range(stages)]
    others = [lax.rem(group + s, groups) for s in range(1, groups)]
    barrier = pltpu.get_barrier_semaphore()
    for device in partners + [(me, other) for other in others]:
        pl.semaphore_signal(
            barrier, inc=1, device_id=device, device_id_type=pl.DeviceIdType.MESH
        )
    pl.semaphore_wait(barrier, stages + groups - 1)

    pieces = []
    order = [0] + list(range(1, stages))
    swapped = [0] + list(range(stages - 1, 0, -1))
    at = 0
    for source, out in ((wide_ref, wide_out), (mid_ref, mid_out)):
        for begin in range(0, source.shape[-1], PIECE):
            path = order if len(pieces) % 2 == 0 else swapped
            pieces.append((source, begin, out, begin, got_big, sum_big, last_big, at, PIECE, path))
            at += PIECE
    pieces.append(
        (thin_ref, 0, thin_out, 0, got_thin, sum_thin, last_thin, 0, thin_ref.shape[-1], order)
    )
    pieces = pieces[-1:] + pieces[:-1]
    started = []

    def begin_stage(number, stage):
        source, begin, _, _, got, total, _, at, width, path = pieces[number]
        left = [b for b in range(stages - 1, -1, -1) if b not in path[:stage]]
        place = left.index(path[stage])
        bit = bits[path[stage]]
        ref, column = (source, begin) if stage == 0 else (total[stage - 1], at)
        index = [slice(None)] * len(left) + [slice(None), pl.ds(column, width)]
        index[place] = 1 - bit
        copy = pltpu.make_async_remote_copy(
            src_ref=ref.at[tuple(index)],
            dst_ref=got[stage].at[
                tuple([slice(None)] * (len(left) - 1) + [slice(None), pl.ds(at, width)])
            ],
            send_sem=send_sem.at[number, stage],
            recv_sem=recv_sem.at[number, stage],
            device_id=partners[path[stage]],
            device_id_type=pl.DeviceIdType.MESH,
        )
        copy.start()
        started.append(copy)
        return copy, ref, column, place, bit, len(left) - 1

    def end_stage(number, stage, state):
        copy, ref, column, place, bit, outer = state
        _, _, _, _, got, total, last, at, width, _ = pieces[number]
        copy.wait_recv()
        rows = ref.shape[-2]
        share = rows // groups
        final = stage == stages - 1
        for combo in range(2**outer):
            lead = [(combo >> (outer - 1 - n)) % 2 for n in range(outer)]
            mine = lead[:place] + [bit] + lead[place:]

            def body(r, carry):
                span = pl.ds(pl.multiple_of(r * share, share), share)
                added = ref[tuple(mine + [span, pl.ds(column, width)])].astype(
                    jnp.float32
                ) + got[stage][tuple(lead + [span, pl.ds(at, width)])].astype(jnp.float32)
                if final:
                    last[r, :, pl.ds(at, width)] = added.astype(last.dtype)
                else:
                    total[stage][tuple(lead + [span, pl.ds(at, width)])] = added.astype(
                        total[stage].dtype
                    )
                return carry

            lax.fori_loop(0, groups, body, 0)

    states = [begin_stage(number, 0) for number in range(len(pieces))]
    for stage in range(stages):
        for number in range(len(pieces)):
            end_stage(number, stage, states[number])
            if stage + 1 < stages:
                states[number] = begin_stage(number, stage + 1)
            else:
                copies = []
                _, _, _, _, got, _, last, at, width, _ = pieces[number]
                landing = rest[4 * stages + 4 + (1 if got is got_thin else 0)]
                for s, other in enumerate(others):
                    copy = pltpu.make_async_remote_copy(
                        src_ref=last.at[other, :, pl.ds(at, width)],
                        dst_ref=landing.at[s, :, pl.ds(at, width)],
                        send_sem=send_sem.at[number, stages + s],
                        recv_sem=recv_sem.at[number, stages + s],
                        device_id=(me, other),
                        device_id_type=pl.DeviceIdType.MESH,
                    )
                    copy.start()
                    started.append(copy)
                    copies.append(copy)
                states[number] = (copies, landing)
    for number in range(len(pieces)):
        copies, landing = states[number]
        _, begin, out, _, _, _, last, at, width, _ = pieces[number]
        added = last[group, :, pl.ds(at, width)].astype(jnp.float32)
        for s, copy in enumerate(copies):
            copy.wait_recv()
            added = added + landing[s, :, pl.ds(at, width)].astype(jnp.float32)
        out[:, pl.ds(begin, width)] = added
    for copy in started:
        copy.wait_send()


def sum_kernel_entry(peers, groups, wide, mid, thin, wide_out, mid_out, thin_out, *rest):
    stages = peers.bit_length() - 1
    body, (land_big, land_thin, send_sem, recv_sem) = rest[:-4], rest[-4:]
    sum_kernel(
        peers,
        groups,
        wide,
        mid,
        thin,
        wide_out,
        mid_out,
        thin_out,
        *body[: 4 * stages + 2],
        send_sem,
        recv_sem,
        land_big,
        land_thin,
    )


def summed_shares(peers, groups, wide, mid, thin):
    stages = peers.bit_length() - 1
    rows = wide.shape[0] // peers
    share = rows // groups
    columns = wide.shape[1] + mid.shape[1]
    lead = (2,) * stages
    count = columns // PIECE + 1
    last_type = jnp.bfloat16 if share % 16 == 0 else jnp.float32
    thin_columns = thin.shape[1]
    scratch = []
    for dtype, size in ((jnp.bfloat16, columns), (jnp.float32, thin_columns)):
        for _ in range(2):
            for stage in range(stages):
                scratch.append(pltpu.VMEM((2,) * (stages - 1 - stage) + (rows, size), dtype))
    scratch += [
        pltpu.VMEM((groups, share, columns), last_type),
        pltpu.VMEM((groups, share, thin_columns), jnp.float32),
        pltpu.VMEM((groups - 1, share, columns), last_type),
        pltpu.VMEM((groups - 1, share, thin_columns), jnp.float32),
        pltpu.SemaphoreType.DMA((count, stages + groups - 1)),
        pltpu.SemaphoreType.DMA((count, stages + groups - 1)),
    ]
    vmem = pl.BlockSpec(memory_space=pltpu.VMEM)
    return pl.pallas_call(
        functools.partial(sum_kernel_entry, peers, groups),
        in_specs=[vmem] * 3,
        out_specs=[vmem] * 3,
        out_shape=[
            jax.ShapeDtypeStruct((share, size), jnp.float32)
            for size in (wide.shape[1], mid.shape[1], thin_columns)
        ],
        scratch_shapes=scratch,
        compiler_params=pltpu.CompilerParams(
            collective_id=0, has_side_effects=True, vmem_limit_bytes=48 * 2**20
        ),
        name="summed_shares",
    )(
        wide.reshape(lead + (rows, wide.shape[1])),
        mid.reshape(lead + (rows, mid.shape[1])),
        thin.reshape(lead + (rows, thin_columns)),
    )


def standardise(values):
    centered = values - jnp.mean(values, axis=1, keepdims=True)
    scale = lax.rsqrt(jnp.mean(centered * centered, axis=1, keepdims=True) + EPS)
    return (centered * scale, scale)


def depth_forward(values, segment, kernel):
    width = kernel.shape[0]
    half = width // 2
    rows = values.shape[0]
    padded = jnp.pad(values, ((half, half), (0, 0)))
    labels = jnp.pad(segment, (half, half), constant_values=-1)
    total = jnp.zeros(values.shape, jnp.float32)
    for offset in range(width):
        same = labels[offset : offset + rows] == segment
        total = (
            total + jnp.where(same[:, None], padded[offset : offset + rows], 0.0) * kernel[offset]
        )
    return total


def depth_backward(values, grad_depth, segment, kernel):
    width = kernel.shape[0]
    half = width // 2
    rows = values.shape[0]
    padded = jnp.pad(values, ((half, half), (0, 0)))
    padded_grad = jnp.pad(grad_depth, ((half, half), (0, 0)))
    labels = jnp.pad(segment, (half, half), constant_values=-1)
    grad_in = jnp.zeros(values.shape, jnp.float32)
    kernel_rows = []
    for offset in range(width):
        same = labels[offset : offset + rows] == segment
        shifted = jnp.where(same[:, None], padded[offset : offset + rows], 0.0)
        kernel_rows.append(jnp.sum(shifted * grad_depth, axis=0))
        back = 2 * half - offset
        same_back = labels[back : back + rows] == segment
        grad_in = (
            grad_in
            + jnp.where(same_back[:, None], padded_grad[back : back + rows], 0.0) * kernel[offset]
        )
    return (grad_in, jnp.stack(kernel_rows, axis=0))


def module(
    hidden_in,
    row_mask,
    segment,
    cotangent,
    pre_gain,
    expand_weight,
    depth_kernel,
    mid_gain,
    output_weight,
    settle,
):
    width = hidden_in.shape[1]
    hidden = hidden_in.astype(jnp.float32)
    normed_in = standardise(hidden)[0]
    norm_in = (normed_in * pre_gain).astype(jnp.bfloat16)
    expanded = product(norm_in, expand_weight)
    value = expanded[:, :width]
    gate = jax.nn.sigmoid(expanded[:, width:])
    gated = value * gate * row_mask[:, None]
    depth_out = depth_forward(gated, segment, depth_kernel)
    normed_mid, scale_mid = standardise(depth_out)
    scaled_mid = normed_mid * mid_gain
    sigma = jax.nn.sigmoid(scaled_mid)
    swish = (scaled_mid * sigma).astype(jnp.bfloat16)
    encoded = ((hidden + product(swish, output_weight)) * row_mask[:, None]).astype(jnp.bfloat16)
    grad_out = jnp.where(row_mask[:, None] > 0, cotangent, jnp.zeros((), cotangent.dtype))
    output_grad = over_rows(swish, grad_out)
    grad_swish = against(grad_out, output_weight)
    grad_scaled = grad_swish * (sigma + scaled_mid * sigma * (1.0 - sigma))
    midnorm_grad = jnp.sum(grad_scaled * normed_mid, axis=0)
    settled = settle(output_grad, midnorm_grad)
    excess = grad_scaled * mid_gain
    grad_depth = scale_mid * (
        excess
        - jnp.mean(excess, axis=1, keepdims=True)
        - normed_mid * jnp.mean(excess * normed_mid, axis=1, keepdims=True)
    )
    grad_gated, kernel_grad = depth_backward(gated, grad_depth, segment, depth_kernel)
    grad_gated = grad_gated * row_mask[:, None]
    grad_expanded = jnp.concatenate(
        [grad_gated * gate, grad_gated * value * gate * (1.0 - gate)], axis=1
    ).astype(jnp.bfloat16)
    expand_grad = over_rows(norm_in, grad_expanded)
    grad_norm = against(grad_expanded, expand_weight)
    prenorm_grad = jnp.sum(grad_norm * normed_in, axis=0)
    return (encoded, (expand_grad, kernel_grad, prenorm_grad), settled)


def gather_half(shard, peers):
    count, columns = shard.shape
    bits = list(range(1, peers.bit_length() - 1))

    def over_plane(piece, path):
        held = piece[None]
        masks = [0]
        for bit in path:
            got = lax.ppermute(held, "dp", [(p, p ^ (1 << bit)) for p in range(peers)])
            held = jnp.concatenate([held, got], axis=0)
            masks = masks + [mask ^ (1 << (bit - 1)) for mask in masks]
        return held, masks

    def over_group(piece):
        return lax.all_gather(piece, "group", axis=0, tiled=False)

    cut = count * 3 // 10
    rest = count // 2 - cut
    bounds = [0, cut, 2 * cut, 2 * cut + rest, count]
    paths = [bits, bits[::-1]]
    lined = over_group(shard[: bounds[2]])
    parts = []
    for n in range(2):
        held, masks = over_plane(lined[:, bounds[n] : bounds[n + 1]], paths[n])
        parts.append([held[masks.index(mask)] for mask in range(peers // 2)])
    flat = []
    for n in range(2, 4):
        held, masks = over_plane(shard[bounds[n] : bounds[n + 1]], paths[n - 2])
        flat.append((held, masks))
    late = over_group(jnp.concatenate([held for held, _ in flat], axis=1))
    at = 0
    for held, masks in flat:
        size = held.shape[1]
        parts.append(
            [late[:, masks.index(mask), at : at + size] for mask in range(peers // 2)]
        )
        at += size
    rows = [
        jnp.concatenate([part[mask] for part in parts], axis=1) for mask in range(peers // 2)
    ]
    return jnp.concatenate(rows, axis=0).reshape(-1, columns)


def per_device(
    frames,
    lengths,
    targets,
    offsets,
    first_filter,
    second_filter,
    projection,
    pre_gain,
    expand_weight,
    depth_kernel,
    mid_gain,
    output_weight,
    cotangent,
):
    peers = lax.axis_size("dp")
    stored = frames[0]
    sizes = lengths[0]
    routes = targets[0]
    starts_at = offsets[0]
    blocks_used = (sizes + FB - 1) // FB
    first_stored = jnp.cumsum(blocks_used) - blocks_used
    match = ((routes[:, None] == jnp.arange(peers)[None, :]) & (sizes[:, None] > 0)).astype(
        jnp.int32
    )
    send_blocks = jnp.sum(match * blocks_used[:, None], axis=0)
    send_first = jnp.sum(match * first_stored[:, None], axis=0)
    send_offset = jnp.sum(match * starts_at[:, None], axis=0)
    send_length = jnp.sum(match * sizes[:, None], axis=0)
    within = jnp.arange(CAP)
    used = within[None, :] < send_blocks[:, None]
    source_rows = jnp.clip(send_first[:, None] + within[None, :], 0, stored.shape[0] - 1)
    outgoing = jnp.take(stored, source_rows.reshape(-1), axis=0).reshape(
        peers, CAP, stored.shape[1]
    )
    labels = jnp.stack(
        [
            jnp.where(used, send_offset[:, None] + within[None, :], -1),
            jnp.where(used, jnp.clip(send_length[:, None] - within[None, :] * FB, 0, FB), 0),
            jnp.broadcast_to(send_offset[:, None], (peers, CAP)),
        ],
        axis=2,
    )
    incoming, arrived = (
        lax.all_to_all(outgoing, "dp", split_axis=0, concat_axis=0, tiled=True),
        lax.all_to_all(labels, "dp", split_axis=0, concat_axis=0, tiled=True),
    )
    received = incoming.reshape(peers * CAP, stored.shape[1])
    tags = arrived.reshape(peers * CAP, 3)
    placing = tags[None, :, 0] == jnp.arange(R_DEV)[:, None]
    blocks = jnp.dot(
        placing.astype(jnp.bfloat16), received, preferred_element_type=jnp.float32
    ).astype(jnp.bfloat16)
    placing_count = placing.astype(jnp.int32)
    valid_frames = jnp.sum(placing_count * tags[None, :, 1], axis=1)
    first_slot = jnp.sum(placing_count * tags[None, :, 2], axis=1)
    is_first = first_slot == jnp.arange(R_DEV)
    groups = lax.axis_size("group")
    width = projection.shape[0] * groups
    features, row_mask = subsample(
        blocks, valid_frames, is_first, first_filter, second_filter, width
    )
    half_weight = gather_half(projection, peers)
    place = lax.axis_index("dp")
    side = place % 2
    swap = [(p, p ^ 1) for p in range(peers)]
    blocks_in = [place // 2 ^ mask for mask in range(peers // 2)]

    def arranged(half):
        taken = [
            lax.dynamic_slice(features, (half, 0, block * width), (1, features.shape[1], width))[0]
            for block in blocks_in
        ]
        return jnp.concatenate(taken, axis=1)

    mine = arranged(side)
    theirs = lax.ppermute(arranged(1 - side), "dp", swap)
    kept = product(mine, half_weight)
    sent = lax.ppermute(product(theirs, half_weight), "dp", swap)
    hidden_in = (kept + sent).astype(jnp.bfloat16)
    hidden_in = hidden_in.reshape(FS, R_DEV, -1).transpose(1, 0, 2).reshape(hidden_in.shape)
    segment = jnp.repeat(first_slot, FS)

    def settle(output_term, midnorm_term):
        return (output_term, midnorm_term)

    encoded, rest, settled = module(
        hidden_in,
        row_mask,
        segment,
        cotangent[0],
        pre_gain,
        expand_weight,
        depth_kernel,
        mid_gain,
        output_weight,
        settle,
    )
    taps = rest[1].shape[0]
    thin = jnp.concatenate([rest[1], rest[2][None], settled[1][None]], axis=0)
    thin = jnp.pad(thin, ((0, LANES - taps - 2), (0, 0))).T
    wide, mid, thin = summed_shares(
        peers,
        lax.axis_size("group"),
        rest[0].astype(jnp.bfloat16),
        settled[0].astype(jnp.bfloat16),
        thin,
    )
    small = thin.T
    return (encoded[None], wide, mid, small[:taps], small[taps], small[taps + 1])


def solution(mesh):
    return jax.shard_map(
        per_device,
        mesh=mesh,
        in_specs=(
            P("group", "dp", None),
            P("group", "dp"),
            P("group", "dp"),
            P("group", "dp"),
            P(),
            P(),
            P(("dp", "group"), None),
            P(),
            P(),
            P(),
            P(),
            P(),
            P("group", "dp", None),
        ),
        out_specs=(
            P("group", "dp", None),
            P(("dp", "group"), None),
            P(("dp", "group"), None),
            P(None, ("dp", "group")),
            P(("dp", "group")),
            P(("dp", "group")),
        ),
        check_vma=False,
    )
```
